32 devices in a mesh: seq: 4 (over y, x), rep: 8 (over z, core).
Axes of the slice: x: 2, y: 2, z: 4, core: 2. Of those that a mesh axis runs over, the one named last changes fastest.
Arguments:
- long_input: bfloat16 [8, 2, 1024, 768], P('rep', None, 'seq'), may hold values from -6 to 6
- short_input: bfloat16 [8, 512, 768], P('rep', 'seq'), may hold values from -6 to 6
- long_cotangent: bfloat16 [8, 2, 1024, 768], P('rep', None, 'seq'), may hold values from -6 to 6
- short_cotangent: bfloat16 [8, 512, 768], P('rep', 'seq'), may hold values from -6 to 6
- doc_lengths: int32 [8, 4], P('rep'), may hold values from 1 to 256, 512 in all within a row
- master_attend: float32 [768, 2304], P('seq', 'rep'), may hold values from -0.21875 to 0.21875
- master_merge: float32 [768, 768], P('seq', 'rep'), may hold values from -0.875 to 0.875
- master_expand: float32 [768, 3072], P('seq', 'rep'), may hold values from -0.21875 to 0.21875
- master_contract: float32 [3072, 768], P('seq', 'rep'), may hold values from -0.109375 to 0.109375
- momentum_attend: float32 [768, 2304], P('seq', 'rep'), may hold values from -3.5 to 3.5
- momentum_merge: float32 [768, 768], P('seq', 'rep'), may hold values from -3.5 to 3.5
- momentum_expand: float32 [768, 3072], P('seq', 'rep'), may hold values from -8 to 8
- momentum_contract: float32 [3072, 768], P('seq', 'rep'), may hold values from -4 to 4
- error_attend: float32 [8, 768, 2304], P('rep', 'seq'), may hold values from -64 to 64
- error_merge: float32 [8, 768, 768], P('rep', 'seq'), may hold values from -64 to 64
- error_expand: float32 [8, 768, 3072], P('rep', 'seq'), may hold values from -160 to 160
- error_contract: float32 [8, 3072, 768], P('rep', 'seq'), may hold values from -160 to 160
- factor_attend: float32 [2304, 8], replicated, may hold values from -4 to 4
- factor_merge: float32 [768, 8], replicated, may hold values from -4 to 4
- factor_expand: float32 [3072, 8], replicated, may hold values from -4 to 4
- factor_contract: float32 [768, 8], replicated, may hold values from -4 to 4
- vector_params: float32 [9216], replicated, may hold values from -0.8 to 1.4, as said below
- vector_momentum: float32 [9216], replicated, may hold values from -56 to 56
Outputs:
- long_output: float32 [8, 2, 1024, 768], P('rep', None, 'seq')
- short_output: float32 [8, 512, 768], P('rep', 'seq')
- long_grad: float32 [8, 2, 1024, 768], P('rep', None, 'seq')
- short_grad: float32 [8, 512, 768], P('rep', 'seq')
- updated_attend: float32 [768, 2304], P('seq', 'rep')
- updated_merge: float32 [768, 768], P('seq', 'rep')
- updated_expand: float32 [768, 3072], P('seq', 'rep')
- updated_contract: float32 [3072, 768], P('seq', 'rep')
- momenta_attend: float32 [768, 2304], P('seq', 'rep')
- momenta_merge: float32 [768, 768], P('seq', 'rep')
- momenta_expand: float32 [768, 3072], P('seq', 'rep')
- momenta_contract: float32 [3072, 768], P('seq', 'rep')
- errors_attend: float32 [8, 768, 2304], P('rep', 'seq')
- errors_merge: float32 [8, 768, 768], P('rep', 'seq')
- errors_expand: float32 [8, 768, 3072], P('rep', 'seq')
- errors_contract: float32 [8, 3072, 768], P('rep', 'seq')
- factors_attend: float32 [2304, 8], replicated
- factors_merge: float32 [768, 8], replicated
- factors_expand: float32 [3072, 8], replicated
- factors_contract: float32 [768, 8], replicated
- updated_vectors: float32 [9216], replicated
- momenta_vectors: float32 [9216], replicated
The draws below stay inside these ranges and needn't reach their ends.
Inputs may be any that keep to these rules, and one draw needn't show every extreme that they name: `doc_lengths`: each replica's 4 lengths sum to 512, and the largest of them is 256. `vector_params`: gain_one and gain_two lie in 0.6 to 1.4, the biases in -0.8 to 0.8.
All inputs are finite; a program needn't handle non-finite values.
Results may differ from the reference program's by a relative error of at most 0.014.
Values may be sent and summed in bfloat16 or wider, within the bound.
No kernel may reach another device: no remote copies, remote signals or barrier semaphores. Data moves between devices by JAX's collectives and lax.ppermute only.
A program may use at most 320 MiB of HBM per device.

```python
import math
import jax
import jax.numpy as jnp
import numpy as np
from jax import lax

D = 768
HEADS = 12
HDIM = 64
FF = 3072
LONG = 1024
LSEQ = 2
SHORT_MOST = 256
SHORT_TOK = 512
DOCS = 4
RANK = 8
REPS = 8
TOK_REP = 2560
SMALL = 9216
N_REP = 8


def draw_vector_params(key, part):
    key_bias = jax.random.fold_in(key, 11)
    key_gain = jax.random.fold_in(key, 12)
    key_tail = jax.random.fold_in(key, 13)
    biases = jnp.clip(jax.random.normal(key_bias, (8, D), jnp.float32), -4.0, 4.0) * 0.2
    gains = jax.random.uniform(key_gain, (8, D), jnp.float32, minval=0.6, maxval=1.4)
    row_ids = jnp.arange(8, dtype=jnp.int32)[:, None]
    is_gain = (row_ids == 0) | (row_ids == 5)
    head = jnp.where(is_gain, gains, biases).reshape(-1)
    tail = jnp.clip(jax.random.normal(key_tail, (FF,), jnp.float32), -4.0, 4.0) * 0.2
    return jnp.concatenate([head, tail]).astype(jnp.float32)


def block_levels(rng, extent, cuts, smallest, high):
    level = 1.0
    for axis_at, blocks in cuts:
        draws = jax.random.uniform(jax.random.fold_in(jax.random.fold_in(rng, 6), axis_at), (blocks,), jnp.float32, smallest / len(cuts), high / len(cuts))
        level = level * jnp.repeat(jnp.exp(draws), extent[axis_at] // blocks).reshape((-1,) + (1,) * (len(extent) - 1 - axis_at))
    return level


def length_profile(number_of, total, limit, lean):
    weights = [(1 << 20) // math.isqrt(rank ** lean) + 1 for rank in range(2, number_of + 1)]
    surplus, holding = total - limit - (number_of - 1), [1] * (number_of - 1)
    while surplus > 0:
        movable = [i for i in range(number_of - 1) if holding[i] < limit]
        mass, budget = sum([weights[i] for i in movable]), surplus
        for i in movable:
            addition = min(limit - holding[i], max(1, budget * weights[i] // mass), surplus)
            holding[i] = holding[i] + addition
            surplus = surplus - addition
    return np.array([limit] + holding)


def ragged(rng, count, total, reach, skew):
    if count == 2:
        one = jax.random.randint(rng, (), max(1, total - reach), min(reach, total - 1) + 1)
        return jnp.stack([one, total - one])
    sizes = jnp.asarray(length_profile(count, total, reach, skew), jnp.int32)
    couples = (count - 1) // 2
    giver, receiver = sizes[1:1 + 2 * couples:2], sizes[2:2 + 2 * couples:2]
    slack = jnp.minimum(giver - 1, reach - receiver)
    moved = jax.random.randint(jax.random.fold_in(rng, 1), (couples,), 0, 1 << 20) % (slack + 1)
    sizes = sizes.at[1:1 + 2 * couples:2].set(giver - moved).at[2:2 + 2 * couples:2].set(receiver + moved)
    return sizes[jax.random.permutation(jax.random.fold_in(rng, 2), count)]


def bell_draw(stream_key, dims, deviation, reach, split=(), held_as=jnp.bfloat16):
    level = block_levels(stream_key, dims, split, -0.22, 0.18) if split else 1.0
    entries = jax.random.normal(stream_key, dims, jnp.float32) * deviation * level
    return jnp.minimum(jnp.maximum(entries, -reach), reach).astype(held_as)


def setup_inputs(seed: int = 0) -> dict:
    arg_keys = jax.random.split(jax.random.key(seed), 24)
    long_input = bell_draw(arg_keys[0], (REPS, LSEQ, LONG, D), 1.0, 6.0, ((0, 8), (2, 4)))
    short_input = bell_draw(arg_keys[1], (REPS, SHORT_TOK, D), 1.0, 6.0, ((0, 8), (1, 4)))
    long_cotangent = bell_draw(arg_keys[2], (REPS, LSEQ, LONG, D), 1.0, 6.0, ((0, 8), (2, 4)))
    short_cotangent = bell_draw(arg_keys[3], (REPS, SHORT_TOK, D), 1.0, 6.0, ((0, 8), (1, 4)))
    doc_lengths = jax.vmap(lambda own: ragged(own, DOCS, SHORT_TOK, SHORT_MOST, 2))(jax.random.split(arg_keys[4], REPS)).reshape((REPS, DOCS)).astype(jnp.int32)
    master_attend = bell_draw(arg_keys[5], (D, 3 * D), D ** -0.5, 0.21875, ((0, 4), (1, 8)), jnp.float32)
    master_merge = bell_draw(arg_keys[6], (D, D), (D // 16) ** -0.5, 0.875, ((0, 4), (1, 8)), jnp.float32)
    master_expand = bell_draw(arg_keys[7], (D, FF), D ** -0.5, 0.21875, ((0, 4), (1, 8)), jnp.float32)
    master_contract = bell_draw(arg_keys[8], (FF, D), FF ** -0.5, 0.109375, ((0, 4), (1, 8)), jnp.float32)
    momentum_attend = bell_draw(arg_keys[9], (D, 3 * D), (0.3 * (TOK_REP * RANK) ** 0.5 * (D * REPS) ** -0.5), 3.5, ((0, 4), (1, 8)), jnp.float32)
    momentum_merge = bell_draw(arg_keys[10], (D, D), (0.3 * (TOK_REP * RANK) ** 0.5 * (D * REPS) ** -0.5), 3.5, ((0, 4), (1, 8)), jnp.float32)
    momentum_expand = bell_draw(arg_keys[11], (D, FF), (0.7 * (TOK_REP * RANK) ** 0.5 * (D * REPS) ** -0.5), 8.0, ((0, 4), (1, 8)), jnp.float32)
    momentum_contract = bell_draw(arg_keys[12], (FF, D), (0.7 * (TOK_REP * RANK) ** 0.5 * (FF * REPS) ** -0.5), 4.0, ((0, 4), (1, 8)), jnp.float32)
    error_attend = bell_draw(arg_keys[13], (REPS, D, 3 * D), (0.2 * TOK_REP ** 0.5), 64.0, ((0, 8), (1, 4)), jnp.float32)
    error_merge = bell_draw(arg_keys[14], (REPS, D, D), (0.2 * TOK_REP ** 0.5), 64.0, ((0, 8), (1, 4)), jnp.float32)
    error_expand = bell_draw(arg_keys[15], (REPS, D, FF), (0.5 * TOK_REP ** 0.5), 160.0, ((0, 8), (1, 4)), jnp.float32)
    error_contract = bell_draw(arg_keys[16], (REPS, FF, D), (0.5 * TOK_REP ** 0.5), 160.0, ((0, 8), (1, 4)), jnp.float32)
    factor_attend = bell_draw(arg_keys[17], (3 * D, RANK), 1.0, 4.0, (), jnp.float32)
    factor_merge = bell_draw(arg_keys[18], (D, RANK), 1.0, 4.0, (), jnp.float32)
    factor_expand = bell_draw(arg_keys[19], (FF, RANK), 1.0, 4.0, (), jnp.float32)
    factor_contract = bell_draw(arg_keys[20], (D, RANK), 1.0, 4.0, (), jnp.float32)
    vector_params = draw_vector_params(jax.random.fold_in(arg_keys[23], 71), 0)
    vector_momentum = bell_draw(arg_keys[22], (SMALL,), (0.5 * (TOK_REP // REPS) ** 0.5), 56.0, (), jnp.float32)
    return {"long_input": long_input, "short_input": short_input, "long_cotangent": long_cotangent, "short_cotangent": short_cotangent, "doc_lengths": doc_lengths, "master_attend": master_attend, "master_merge": master_merge, "master_expand": master_expand, "master_contract": master_contract, "momentum_attend": momentum_attend, "momentum_merge": momentum_merge, "momentum_expand": momentum_expand, "momentum_contract": momentum_contract, "error_attend": error_attend, "error_merge": error_merge, "error_expand": error_expand, "error_contract": error_contract, "factor_attend": factor_attend, "factor_merge": factor_merge, "factor_expand": factor_expand, "factor_contract": factor_contract, "vector_params": vector_params, "vector_momentum": vector_momentum}


LN_EPS = 1e-05
NORM_EPS = 1e-06
BETA = 0.9
RATE_MATRIX = 0.1
RATE_VECTOR = 0.01
MASKED = -1e+30
HIGH = lax.Precision.HIGHEST

@jax.custom_vjp
def low(v):
    return lax.optimization_barrier(v.astype(jnp.bfloat16)).astype(jnp.float32)

@jax.custom_vjp
def low_back(v):
    return v

def low_keep(v):
    return (low(v), None)

def low_pass(kept, grad):
    return (grad,)

def back_keep(v):
    return (v, None)

def back_low(kept, grad):
    return (low(grad),)
low.defvjp(low_keep, low_pass)
low_back.defvjp(back_keep, back_low)

def layer_norm(values, gain, shift):
    center = values - lax.optimization_barrier(jnp.mean(values, axis=-1, keepdims=True))
    spread = lax.optimization_barrier(jnp.mean(center * center, axis=-1, keepdims=True))
    return center * lax.rsqrt(spread + LN_EPS) * gain + shift

def matmul(left, right):
    return jnp.einsum('btd,de->bte', left, right, precision=HIGH)

def unpack(vectors):
    head = vectors[:8 * D].reshape(8, D)
    return (head[0], head[1], head[2], head[3], head[4], head[5], head[6], head[7], vectors[8 * D:])

def orthonormal(matrix):
    columns = []
    for column_id in range(matrix.shape[1]):
        column = matrix[:, column_id]
        for earlier in columns:
            column = column - jnp.sum(earlier * column) * earlier
        column = column * lax.rsqrt(jnp.sum(column * column) + NORM_EPS)
        columns.append(column)
    return jnp.stack(columns, axis=1)

def attention(normed, w_attend, w_merge, bias_query, bias_value, bias_merge, allowed):
    batch, length = (normed.shape[0], normed.shape[1])
    shape_heads = (batch, length, HEADS, HDIM)
    joined = low_back(matmul(normed, w_attend))
    queries = low(joined[..., :D] + bias_query).reshape(shape_heads)
    keys = low(joined[..., D:2 * D]).reshape(shape_heads)
    values = low(joined[..., 2 * D:] + bias_value).reshape(shape_heads)
    raw_scores = low_back(jnp.einsum('bqhd,bkhd->bhqk', queries, keys, precision=HIGH))
    scores = jnp.where(allowed, raw_scores * HDIM ** (-0.5), MASKED)
    soft = low(jax.nn.softmax(scores, axis=-1))
    mixed = low(low_back(jnp.einsum('bhqk,bkhd->bqhd', soft, values, precision=HIGH)))
    return low_back(matmul(mixed.reshape(batch, length, D), w_merge)) + bias_merge

def block(inputs, w_attend, w_merge, w_expand, w_contract, vectors, allowed):
    gain_one, shift_one, bias_query, bias_value, bias_merge, gain_two, shift_two, bias_contract, bias_expand = unpack(vectors)
    normed = low(layer_norm(inputs, gain_one, shift_one))
    middle = inputs + attention(normed, w_attend, w_merge, bias_query, bias_value, bias_merge, allowed)
    hidden = low(layer_norm(middle, gain_two, shift_two))
    expanded = low_back(matmul(hidden, w_expand)) + bias_expand
    activated = low(jax.nn.gelu(expanded, approximate=True))
    return middle + low_back(matmul(activated, w_contract)) + bias_contract

def replica_grads(weights, vectors, long_x, short_x, long_dy, short_dy, lengths):
    positions_long = jnp.arange(LONG, dtype=jnp.int32)
    causal_long = positions_long[None, :] <= positions_long[:, None]
    positions_short = jnp.arange(SHORT_TOK, dtype=jnp.int32)
    doc_ends = jnp.cumsum(lengths)
    document = lax.optimization_barrier(jnp.sum((positions_short[:, None] >= doc_ends[None, :]).astype(jnp.int32), axis=1))
    causal_short = (positions_short[None, :] <= positions_short[:, None]) & (document[None, :] == document[:, None])

    def forward(w_attend, w_merge, w_expand, w_contract, vectors_in, long_in, short_in):
        long_out = block(long_in, w_attend, w_merge, w_expand, w_contract, vectors_in, causal_long)
        short_out = block(short_in[None], w_attend, w_merge, w_expand, w_contract, vectors_in, causal_short)[0]
        return (long_out, short_out)
    outputs, pullback = jax.vjp(forward, weights[0], weights[1], weights[2], weights[3], vectors, long_x, short_x)
    grads = pullback((long_dy, short_dy))
    return (outputs, grads)

def compress(stacked, factor, momentum, master):
    projected = jnp.einsum('rnm,mk->nk', stacked, factor, precision=HIGH) / N_REP
    basis = orthonormal(projected)
    renewed = jnp.einsum('rnm,nk->mk', stacked, basis, precision=HIGH) / N_REP
    approx = jnp.dot(basis, renewed.T, precision=HIGH)
    new_errors = stacked - approx[None]
    new_momentum = BETA * momentum + approx
    return (master - RATE_MATRIX * new_momentum, new_momentum, new_errors, renewed)

def reference(long_input, short_input, long_cotangent, short_cotangent, doc_lengths, master_attend, master_merge, master_expand, master_contract, momentum_attend, momentum_merge, momentum_expand, momentum_contract, error_attend, error_merge, error_expand, error_contract, factor_attend, factor_merge, factor_expand, factor_contract, vector_params, vector_momentum):
    masters = (master_attend, master_merge, master_expand, master_contract)
    weights = tuple((matrix.astype(jnp.bfloat16).astype(jnp.float32) for matrix in masters))

    def one_replica(slices):
        long_x, short_x, long_dy, short_dy, lengths, err_one, err_two, err_three, err_four = slices
        outputs, grads = replica_grads(weights, vector_params, long_x.astype(jnp.float32), short_x.astype(jnp.float32), long_dy.astype(jnp.float32), short_dy.astype(jnp.float32), lengths)
        corrected = (grads[0] + err_one, grads[1] + err_two, grads[2] + err_three, grads[3] + err_four)
        return (outputs[0], outputs[1], grads[5], grads[6], corrected, grads[4])
    results = lax.map(one_replica, (long_input, short_input, long_cotangent, short_cotangent, doc_lengths, error_attend, error_merge, error_expand, error_contract))
    long_out, short_out, long_grad, short_grad, corrected, vector_grads = results
    factors = (factor_attend, factor_merge, factor_expand, factor_contract)
    momenta = (momentum_attend, momentum_merge, momentum_expand, momentum_contract)
    packed = [compress(corrected[number], factors[number], momenta[number], masters[number]) for number in range(4)]
    vector_grad = lax.optimization_barrier(jnp.sum(vector_grads, axis=0)) / N_REP
    momenta_vectors = BETA * vector_momentum + vector_grad
    updated_vectors = vector_params - RATE_VECTOR * momenta_vectors
    return (long_out, short_out, long_grad, short_grad, packed[0][0], packed[1][0], packed[2][0], packed[3][0], packed[0][1], packed[1][1], packed[2][1], packed[3][1], packed[0][2], packed[1][2], packed[2][2], packed[3][2], packed[0][3], packed[1][3], packed[2][3], packed[3][3], updated_vectors, momenta_vectors)
```

```python
from functools import partial

import jax
import jax.numpy as jnp
from jax import lax
from jax.experimental import pallas as pl
from jax.sharding import PartitionSpec as P

D = 768
HEADS = 12
HDIM = 64
LANES = 128


LN_EPS = 1e-05
NORM_EPS = 1e-06
BETA = 0.9
RATE_MATRIX = 0.1
RATE_VECTOR = 0.01
MASKED = -1e30
HIGH = lax.Precision.HIGHEST


def layer_norm(values, gain, shift):
    center = values - jnp.mean(values, axis=-1, keepdims=True)
    spread = jnp.mean(center * center, axis=-1, keepdims=True)
    return center * lax.rsqrt(spread + LN_EPS) * gain + shift


def unpack(vectors):
    head = vectors[: 8 * D].reshape(8, D)
    return (
        head[0],
        head[1],
        head[2],
        head[3],
        head[4],
        head[5],
        head[6],
        head[7],
        vectors[8 * D :],
    )


def orthonormal(gathered, widths, scale):
    rank = gathered.shape[1]

    def kernel(p_ref, basis_ref):
        offset = 0
        for width in widths:
            block = p_ref[:, :, offset : offset + width] * scale
            row_ids = lax.broadcasted_iota(jnp.int32, (1, rank, 1), 1)
            for column_id in range(rank):
                column = block[:, column_id : column_id + 1, :]
                length = jnp.sum(
                    jnp.sum(column * column, axis=2, keepdims=True), axis=0, keepdims=True
                )
                unit = column * lax.rsqrt(length + NORM_EPS)
                inner = jnp.sum(
                    jnp.sum(block * unit, axis=2, keepdims=True), axis=0, keepdims=True
                )
                later = jnp.where(row_ids > column_id, inner, 0.0)
                block = jnp.where(row_ids == column_id, unit, block - later * unit)
            basis_ref[:, :, offset : offset + width] = block
            offset += width

    return pl.pallas_call(
        kernel, out_shape=jax.ShapeDtypeStruct(gathered.shape, jnp.float32), name="orthonormal"
    )(gathered)


def contract_rows(left, right, precision=None):
    return lax.dot_general(
        left,
        right,
        (((0,), (0,)), ((), ())),
        precision=precision,
        preferred_element_type=jnp.float32,
    )


def contract_cols(left, right, precision=None):
    return lax.dot_general(
        left,
        right,
        (((1,), (1,)), ((), ())),
        precision=precision,
        preferred_element_type=jnp.float32,
    )


def run_layer(tokens, cotangent, allowed, weights, vectors):
    w_attend, w_merge, w_expand, w_contract = weights
    (
        gain_one,
        shift_one,
        bias_query,
        bias_value,
        bias_merge,
        gain_two,
        shift_two,
        bias_contract,
        bias_expand,
    ) = unpack(vectors)
    batch, length = (tokens.shape[0], tokens.shape[1])
    rows_all = batch * length
    inputs = tokens.astype(jnp.float32).reshape(rows_all, D)
    normed_one, norm_one_back = jax.vjp(layer_norm, inputs, gain_one, shift_one)
    normed_low = normed_one.astype(jnp.bfloat16)
    joined = jnp.dot(normed_low, w_attend, preferred_element_type=jnp.float32)
    queries = (joined[:, :D] + bias_query).astype(jnp.bfloat16)
    keys_local = joined[:, D : 2 * D].astype(jnp.bfloat16)
    values_local = (joined[:, 2 * D :] + bias_value).astype(jnp.bfloat16)
    keys_all, values_all = (
        lax.all_gather(keys_local.reshape(batch, length, D), "seq", axis=1, tiled=True),
        lax.all_gather(values_local.reshape(batch, length, D), "seq", axis=1, tiled=True),
    )
    span = keys_all.shape[1]
    query_heads = queries.reshape(batch, length, HEADS, HDIM)
    key_heads = keys_all.reshape(batch, span, HEADS, HDIM)
    value_heads = values_all.reshape(batch, span, HEADS, HDIM)
    scale = HDIM ** (-0.5)

    def score_of():
        raw_scores = jnp.einsum(
            "bqhd,bkhd->bhqk", query_heads, key_heads, preferred_element_type=jnp.float32
        )
        return jnp.where(allowed, raw_scores * scale, MASKED)

    scores = score_of()
    row_top = jnp.max(scores, axis=-1, keepdims=True)
    expo = jnp.exp(scores - row_top)
    row_total = jnp.sum(expo, axis=-1, keepdims=True)
    soft_low = (expo / row_total).astype(jnp.bfloat16)
    log_total = row_top + jnp.log(row_total)
    mixed = (
        jnp.einsum("bhqk,bkhd->bqhd", soft_low, value_heads, preferred_element_type=jnp.float32)
        .astype(jnp.bfloat16)
        .reshape(rows_all, D)
    )
    middle = inputs + jnp.dot(mixed, w_merge, preferred_element_type=jnp.float32) + bias_merge
    normed_two, norm_two_back = jax.vjp(layer_norm, middle, gain_two, shift_two)
    hidden = normed_two.astype(jnp.bfloat16)
    expanded = jnp.dot(hidden, w_expand, preferred_element_type=jnp.float32) + bias_expand
    activated, gelu_back = jax.vjp(partial(jax.nn.gelu, approximate=True), expanded)
    active_low = activated.astype(jnp.bfloat16)
    output = (
        middle + jnp.dot(active_low, w_contract, preferred_element_type=jnp.float32) + bias_contract
    )
    grad_out = cotangent.astype(jnp.float32).reshape(rows_all, D)
    grad_out_low = cotangent.reshape(rows_all, D)
    contract_bias_grad = jnp.sum(grad_out, axis=0)
    grad_active = contract_cols(grad_out_low, w_contract)
    (grad_expanded,) = gelu_back(grad_active)
    expand_bias_grad = jnp.sum(grad_expanded, axis=0)
    expanded_low = grad_expanded.astype(jnp.bfloat16)
    grad_hidden = contract_cols(expanded_low, w_expand)
    middle_part, gain_two_grad, shift_two_grad = norm_two_back(grad_hidden)
    grad_middle = grad_out + middle_part
    merge_bias_grad = jnp.sum(grad_middle, axis=0)
    middle_low = grad_middle.astype(jnp.bfloat16)
    grad_mixed = (
        contract_cols(middle_low, w_merge).astype(jnp.bfloat16).reshape(batch, length, HEADS, HDIM)
    )
    soft_again = jnp.exp(score_of() - log_total)
    soft_again_low = soft_again.astype(jnp.bfloat16)
    values_grad_all = jnp.einsum(
        "bhqk,bqhd->bkhd", soft_again_low, grad_mixed, preferred_element_type=jnp.float32
    )
    grad_soft = jnp.einsum(
        "bqhd,bkhd->bhqk", grad_mixed, value_heads, preferred_element_type=jnp.float32
    )
    row_inner = jnp.sum(soft_again * grad_soft, axis=-1, keepdims=True)
    grad_scores = (soft_again * (grad_soft - row_inner) * scale).astype(jnp.bfloat16)
    grad_queries = jnp.einsum(
        "bhqk,bkhd->bqhd", grad_scores, key_heads, preferred_element_type=jnp.float32
    ).reshape(rows_all, D)
    keys_grad_all = jnp.einsum(
        "bhqk,bqhd->bkhd", grad_scores, query_heads, preferred_element_type=jnp.float32
    )
    keys_grad, values_grad = (
        lax.psum_scatter(
            keys_grad_all.reshape(batch, span, D), "seq", scatter_dimension=1, tiled=True
        ),
        lax.psum_scatter(
            values_grad_all.reshape(batch, span, D), "seq", scatter_dimension=1, tiled=True
        ),
    )
    keys_grad = keys_grad.reshape(rows_all, D)
    values_grad = values_grad.reshape(rows_all, D)
    query_bias_grad = jnp.sum(grad_queries, axis=0)
    value_bias_grad = jnp.sum(values_grad, axis=0)
    joined_low = jnp.concatenate([grad_queries, keys_grad, values_grad], axis=1).astype(
        jnp.bfloat16
    )
    grad_normed = contract_cols(joined_low, w_attend)
    input_part, gain_one_grad, shift_one_grad = norm_one_back(grad_normed)
    grad_input = grad_middle + input_part
    vector_grad = jnp.concatenate(
        [
            gain_one_grad,
            shift_one_grad,
            query_bias_grad,
            value_bias_grad,
            merge_bias_grad,
            gain_two_grad,
            shift_two_grad,
            contract_bias_grad,
            expand_bias_grad,
        ]
    )
    operands = (
        normed_low,
        joined_low,
        mixed,
        middle_low,
        hidden,
        expanded_low,
        active_low,
        grad_out_low,
    )
    return (
        output.reshape(batch, length, D),
        grad_input.reshape(batch, length, D),
        operands,
        vector_grad,
    )


def local(
    long_input,
    short_input,
    long_cotangent,
    short_cotangent,
    doc_lengths,
    master_attend,
    master_merge,
    master_expand,
    master_contract,
    momentum_attend,
    momentum_merge,
    momentum_expand,
    momentum_contract,
    error_attend,
    error_merge,
    error_expand,
    error_contract,
    factor_attend,
    factor_merge,
    factor_expand,
    factor_contract,
    vector_params,
    vector_momentum,
):
    masters = (master_attend, master_merge, master_expand, master_contract)
    widened = (
        lax.all_gather(master_attend.astype(jnp.bfloat16), "rep", axis=1, tiled=True),
        lax.all_gather(master_merge.astype(jnp.bfloat16), "rep", axis=1, tiled=True),
        lax.all_gather(master_expand.astype(jnp.bfloat16), "rep", axis=1, tiled=True),
        lax.all_gather(master_contract.astype(jnp.bfloat16), "rep", axis=1, tiled=True),
    )
    weights = (
        lax.all_gather(widened[0], "seq", axis=0, tiled=True),
        lax.all_gather(widened[1], "seq", axis=0, tiled=True),
        lax.all_gather(widened[2], "seq", axis=0, tiled=True),
        lax.all_gather(widened[3], "seq", axis=0, tiled=True),
    )
    seq_index = lax.axis_index("seq")
    seq_count = lax.axis_size("seq")
    rep_index = lax.axis_index("rep")
    rep_count = lax.axis_size("rep")
    long_tokens = long_input[0]
    long_length = long_tokens.shape[1]
    query_long = seq_index * long_length + jnp.arange(long_length, dtype=jnp.int32)
    key_long = jnp.arange(long_length * seq_count, dtype=jnp.int32)
    allowed_long = key_long[None, :] <= query_long[:, None]
    short_length = short_input.shape[1]
    query_short = seq_index * short_length + jnp.arange(short_length, dtype=jnp.int32)
    key_short = jnp.arange(short_length * seq_count, dtype=jnp.int32)
    doc_ends = jnp.cumsum(doc_lengths[0])
    query_doc = jnp.sum((query_short[:, None] >= doc_ends[None, :]).astype(jnp.int32), axis=1)
    key_doc = jnp.sum((key_short[:, None] >= doc_ends[None, :]).astype(jnp.int32), axis=1)
    allowed_short = (key_short[None, :] <= query_short[:, None]) & (
        key_doc[None, :] == query_doc[:, None]
    )
    long_result = run_layer(long_tokens, long_cotangent[0], allowed_long, weights, vector_params)
    short_result = run_layer(short_input, short_cotangent, allowed_short, weights, vector_params)
    operands = tuple(
        (
            jnp.concatenate([long_result[2][number], short_result[2][number]], axis=0)
            for number in range(8)
        )
    )
    local_grads = tuple(
        (contract_rows(operands[2 * number], operands[2 * number + 1]) for number in range(4))
    )
    summed = (
        lax.psum_scatter(
            local_grads[0].astype(jnp.bfloat16), "seq", scatter_dimension=0, tiled=True
        ).astype(jnp.float32),
        lax.psum_scatter(
            local_grads[1].astype(jnp.bfloat16), "seq", scatter_dimension=0, tiled=True
        ).astype(jnp.float32),
        lax.psum_scatter(
            local_grads[2].astype(jnp.bfloat16), "seq", scatter_dimension=0, tiled=True
        ).astype(jnp.float32),
        lax.psum_scatter(
            local_grads[3].astype(jnp.bfloat16), "seq", scatter_dimension=0, tiled=True
        ).astype(jnp.float32),
    )
    errors = (error_attend, error_merge, error_expand, error_contract)
    factors = (factor_attend, factor_merge, factor_expand, factor_contract)
    momenta = (momentum_attend, momentum_merge, momentum_expand, momentum_contract)
    corrected = [summed[number] + errors[number][0] for number in range(4)]
    heights = [corrected[number].shape[0] for number in range(4)]
    padded = [-(-height // LANES) * LANES for height in heights]
    projected = jnp.concatenate(
        [
            jnp.pad(
                lax.dot_general(
                    factors[number],
                    corrected[number],
                    (((0,), (1,)), ((), ())),
                    precision=HIGH,
                    preferred_element_type=jnp.float32,
                ),
                ((0, 0), (0, padded[number] - heights[number])),
            )
            for number in range(4)
        ],
        axis=1,
    )
    reduced = lax.psum(projected, "rep")
    whole_p = lax.all_gather(reduced, "seq", axis=0, tiled=False)
    basis_all = orthonormal(whole_p, padded, 1.0 / rep_count)
    basis_own = lax.dynamic_index_in_dim(basis_all, seq_index, 0, keepdims=False)
    basis_rows = []
    partial_q = []
    offset = 0
    for number in range(4):
        own_rows = basis_own[:, offset : offset + heights[number]]
        offset += padded[number]
        basis_rows.append(own_rows)
        partial_q.append(
            jnp.dot(
                own_rows, corrected[number], precision=HIGH, preferred_element_type=jnp.float32
            )
        )
    rank = projected.shape[0]
    vector_total = long_result[3] + short_result[3]
    renewed_all = lax.psum(
        jnp.concatenate(partial_q + [vector_total.reshape(rank, -1)], axis=1), ("seq", "rep")
    )
    renewed_all = renewed_all / rep_count
    updated = []
    new_momenta = []
    new_errors = []
    new_factors = []
    offset = 0
    for number in range(4):
        columns = corrected[number].shape[1]
        renewed = renewed_all[:, offset : offset + columns]
        offset += columns
        approx = contract_rows(basis_rows[number], renewed, HIGH)
        new_errors.append((corrected[number] - approx)[None])
        width = masters[number].shape[1]
        own_block = lax.dynamic_slice_in_dim(approx, rep_index * width, width, 1)
        momentum_next = BETA * momenta[number] + own_block
        new_momenta.append(momentum_next)
        updated.append(masters[number] - RATE_MATRIX * momentum_next)
        new_factors.append(renewed.T)
    vector_grad = renewed_all[:, offset:].reshape(vector_total.shape)
    momenta_vectors = BETA * vector_momentum + vector_grad
    updated_vectors = vector_params - RATE_VECTOR * momenta_vectors
    long_output = long_result[0].reshape(long_input.shape)
    long_grad = long_result[1].reshape(long_input.shape)
    return (
        long_output,
        short_result[0],
        long_grad,
        short_result[1],
        updated[0],
        updated[1],
        updated[2],
        updated[3],
        new_momenta[0],
        new_momenta[1],
        new_momenta[2],
        new_momenta[3],
        new_errors[0],
        new_errors[1],
        new_errors[2],
        new_errors[3],
        new_factors[0],
        new_factors[1],
        new_factors[2],
        new_factors[3],
        updated_vectors,
        momenta_vectors,
    )


def solution(mesh):
    in_specs = (
        P("rep", None, "seq", None),
        P("rep", "seq", None),
        P("rep", None, "seq", None),
        P("rep", "seq", None),
        P("rep", None),
        P("seq", "rep"),
        P("seq", "rep"),
        P("seq", "rep"),
        P("seq", "rep"),
        P("seq", "rep"),
        P("seq", "rep"),
        P("seq", "rep"),
        P("seq", "rep"),
        P("rep", "seq", None),
        P("rep", "seq", None),
        P("rep", "seq", None),
        P("rep", "seq", None),
        P(),
        P(),
        P(),
        P(),
        P(),
        P(),
    )
    out_specs = (
        P("rep", None, "seq", None),
        P("rep", "seq", None),
        P("rep", None, "seq", None),
        P("rep", "seq", None),
        P("seq", "rep"),
        P("seq", "rep"),
        P("seq", "rep"),
        P("seq", "rep"),
        P("seq", "rep"),
        P("seq", "rep"),
        P("seq", "rep"),
        P("seq", "rep"),
        P("rep", "seq", None),
        P("rep", "seq", None),
        P("rep", "seq", None),
        P("rep", "seq", None),
        P(),
        P(),
        P(),
        P(),
        P(),
        P(),
    )
    return jax.shard_map(local, mesh=mesh, in_specs=in_specs, out_specs=out_specs, check_vma=False)
```

```python
from functools import partial

import jax
import jax.numpy as jnp
from jax import lax
from jax.experimental import pallas as pl
from jax.experimental.pallas import tpu as pltpu
from jax.sharding import PartitionSpec as P

D = 768
HEADS = 12
HDIM = 64
LANES = 128


LN_EPS = 1e-05
NORM_EPS = 1e-06
BETA = 0.9
RATE_MATRIX = 0.1
RATE_VECTOR = 0.01
MASKED = -1e30
HIGH = lax.Precision.HIGHEST


def layer_norm(values, gain, shift):
    center = values - jnp.mean(values, axis=-1, keepdims=True)
    spread = jnp.mean(center * center, axis=-1, keepdims=True)
    return center * lax.rsqrt(spread + LN_EPS) * gain + shift


def unpack(vectors):
    head = vectors[: 8 * D].reshape(8, D)
    return (
        head[0],
        head[1],
        head[2],
        head[3],
        head[4],
        head[5],
        head[6],
        head[7],
        vectors[8 * D :],
    )


def orthonormal(gathered, widths, scale):
    rank = gathered.shape[1]

    def over_pieces(values):
        parts = [values[at : at + 1] for at in range(values.shape[0])]
        while len(parts) > 1:
            parts = [left + right for left, right in zip(parts[::2], parts[1::2])]
        return parts[0]

    def kernel(p_ref, basis_ref):
        offset = 0
        for width in widths:
            block = p_ref[:, :, offset : offset + width] * scale
            row_ids = lax.broadcasted_iota(jnp.int32, (1, rank, 1), 1)
            for column_id in range(rank):
                column = block[:, column_id : column_id + 1, :]
                length = over_pieces(jnp.sum(column * column, axis=2, keepdims=True))
                unit = column * lax.rsqrt(length + NORM_EPS)
                inner = over_pieces(jnp.sum(block * unit, axis=2, keepdims=True))
                later = jnp.where(row_ids > column_id, inner, 0.0)
                block = jnp.where(row_ids == column_id, unit, block - later * unit)
            basis_ref[:, offset : offset + width] = block[0]
            offset += width

    return pl.pallas_call(
        kernel, out_shape=jax.ShapeDtypeStruct(gathered.shape[1:], jnp.float32), name="orthonormal"
    )(gathered)


def contract_rows(left, right, precision=None):
    return lax.dot_general(
        left,
        right,
        (((0,), (0,)), ((), ())),
        precision=precision,
        preferred_element_type=jnp.float32,
    )


def contract_cols(left, right, precision=None):
    return lax.dot_general(
        left,
        right,
        (((1,), (1,)), ((), ())),
        precision=precision,
        preferred_element_type=jnp.float32,
    )


def swap_with(values, axis, distance):
    count = lax.axis_size(axis)
    return lax.ppermute(values, axis, [(source, source ^ distance) for source in range(count)])


def butterfly_sum(values, axis):
    distance = 1
    while distance < lax.axis_size(axis):
        values = values + swap_with(values, axis, distance)
        distance *= 2
    return values


def gather_stacked(values, axis):
    count = lax.axis_size(axis)
    return jnp.stack(
        [values] + [swap_with(values, axis, distance) for distance in range(1, count)]
    )


def halve(blocks, axis_at, distance):
    bit = (lax.axis_index("seq") // distance) % 2
    sent = lax.dynamic_index_in_dim(blocks, 1 - bit, axis_at, keepdims=False)
    kept = lax.dynamic_index_in_dim(blocks, bit, axis_at, keepdims=False)
    received = swap_with(sent, "seq", distance)
    return kept.astype(jnp.float32) + received.astype(jnp.float32)


def scatter_rows(matrix):
    rows, columns = matrix.shape
    if lax.axis_size("seq") != 4:
        return lax.psum_scatter(matrix, "seq", scatter_dimension=0, tiled=True).astype(jnp.float32)
    blocks = matrix.reshape(2, 2, rows // 4, columns)
    middle = columns // 2
    first = halve(blocks[..., :middle], 1, 1).astype(jnp.bfloat16)
    second = halve(blocks[..., middle:], 0, 2).astype(jnp.bfloat16)
    return jnp.concatenate([halve(first, 0, 2), halve(second, 0, 1)], axis=1)


def exchange(values):
    return lax.all_to_all(values, "seq", split_axis=0, concat_axis=0, tiled=True)


def dot_of(left, right, left_dim, right_dim):
    return lax.dot_general(
        left,
        right,
        (((left_dim,), (right_dim,)), ((), ())),
        preferred_element_type=jnp.float32,
    )


def attention_calls(chunks, batch, length, short_length, width, dtype=jnp.bfloat16):
    heads = width // HDIM
    scale = HDIM ** (-0.5)
    rows_all = batch * length + short_length
    smem = pl.BlockSpec(memory_space=pltpu.SMEM)
    vmem = pl.BlockSpec(memory_space=pltpu.VMEM)

    def causal(size):
        key_ids = lax.broadcasted_iota(jnp.int32, (size, size), 0)
        query_ids = lax.broadcasted_iota(jnp.int32, (size, size), 1)
        return key_ids <= query_ids

    def long_mask(scores, key_at, query_at):
        if key_at != query_at:
            return scores
        return jnp.where(causal(length), scores, MASKED)

    def short_mask_of(docs_ref):
        ends = []
        end = 0
        for number in range(docs_ref.shape[1]):
            end = end + docs_ref[0, number]
            ends.append(end)

        def document(position):
            found = jnp.zeros_like(position)
            for end in ends:
                found = found + jnp.where(position >= end, 1, 0)
            return found

        def short_mask(scores, key_at, query_at):
            size = short_length
            key_ids = lax.broadcasted_iota(jnp.int32, (size, 1), 0) + key_at * size
            query_ids = lax.broadcasted_iota(jnp.int32, (1, size), 1) + query_at * size
            allowed = document(key_ids) == document(query_ids)
            if key_at == query_at:
                allowed = allowed & causal(size)
            return jnp.where(allowed, scores, MASKED)

        return short_mask

    def parts_of(ref, first, size, start, head):
        low = start + head * HDIM
        return [ref[chunk, pl.ds(first, size), low : low + HDIM] for chunk in range(chunks)]

    def forward(docs_ref, joined_ref, mixed_ref, long_log_ref, short_log_ref):
        def run(first, size, mask, log_store):
            for query_at in range(chunks):
                pieces = []
                for head in range(heads):
                    low = head * HDIM
                    query = joined_ref[query_at, pl.ds(first, size), low : low + HDIM] * scale
                    keys = parts_of(joined_ref, first, size, width, head)
                    values = parts_of(joined_ref, first, size, 2 * width, head)
                    scores = [
                        mask(dot_of(keys[at], query, 1, 1), at, query_at)
                        for at in range(query_at + 1)
                    ]
                    top = jnp.max(scores[0], axis=0, keepdims=True)
                    for part in scores[1:]:
                        top = jnp.maximum(top, jnp.max(part, axis=0, keepdims=True))
                    expo = [jnp.exp(part - top) for part in scores]
                    total = sum(jnp.sum(part, axis=0, keepdims=True) for part in expo)
                    inverse = 1.0 / total
                    pieces.append(
                        sum(
                            dot_of(values[at], (expo[at] * inverse).astype(dtype), 0, 0)
                            for at in range(query_at + 1)
                        )
                    )
                    log_store(query_at, head, top + jnp.log(total))
                mixed = jnp.concatenate(pieces, axis=0).T
                mixed_ref[query_at, pl.ds(first, size), :] = mixed.astype(dtype)

        def long_step(number, carry):
            def store(query_at, head, log_total):
                long_log_ref[number, query_at, head : head + 1, :] = log_total

            run(pl.multiple_of(number * length, length), length, long_mask, store)
            return carry

        lax.fori_loop(0, batch, long_step, 0)

        def short_store(query_at, head, log_total):
            short_log_ref[query_at, head : head + 1, :] = log_total

        run(batch * length, short_length, short_mask_of(docs_ref), short_store)

    def backward(
        docs_ref, joined_ref, grad_ref, long_log_ref, short_log_ref, out_ref, sums_ref
    ):
        sums_ref[...] = jnp.zeros_like(sums_ref)

        def run(first, size, mask, log_load):
            grad_query = [[] for _ in range(chunks)]
            grad_key = [[] for _ in range(chunks)]
            grad_value = [[] for _ in range(chunks)]
            for head in range(heads):
                keys = parts_of(joined_ref, first, size, width, head)
                values = parts_of(joined_ref, first, size, 2 * width, head)
                queries = parts_of(joined_ref, first, size, 0, head)
                grads = parts_of(grad_ref, first, size, 0, head)
                key_sums = [0.0] * chunks
                value_sums = [0.0] * chunks
                for query_at in range(chunks):
                    query = queries[query_at] * scale
                    grad = grads[query_at]
                    log_total = log_load(query_at, head)
                    soft = []
                    soft_grad = []
                    inner = 0.0
                    for at in range(query_at + 1):
                        scores = mask(dot_of(keys[at], query, 1, 1), at, query_at)
                        soft.append(jnp.exp(scores - log_total))
                        soft_grad.append(dot_of(values[at], grad, 1, 1))
                        inner = inner + jnp.sum(soft[at] * soft_grad[at], axis=0, keepdims=True)
                    query_sum = 0.0
                    for at in range(query_at + 1):
                        score_grad = (soft[at] * (soft_grad[at] - inner)).astype(dtype)
                        query_sum = query_sum + dot_of(keys[at], score_grad, 0, 0)
                        key_sums[at] = key_sums[at] + dot_of(score_grad, query, 1, 0)
                        value_sums[at] = value_sums[at] + dot_of(
                            soft[at].astype(dtype), grad, 1, 0
                        )
                    grad_query[query_at].append(query_sum * scale)
                for at in range(chunks):
                    grad_key[at].append(key_sums[at])
                    grad_value[at].append(value_sums[at])
            for at in range(chunks):
                query_all = jnp.concatenate(grad_query[at], axis=0).T
                value_all = jnp.concatenate(grad_value[at], axis=1)
                sums_ref[0:1, :] += jnp.sum(query_all, axis=0, keepdims=True)
                sums_ref[1:2, :] += jnp.sum(value_all, axis=0, keepdims=True)
                out_ref[at, pl.ds(first, size), :] = jnp.concatenate(
                    [query_all] + grad_key[at] + [value_all], axis=1
                ).astype(dtype)

        def long_step(number, carry):
            def load(query_at, head):
                return long_log_ref[number, query_at, head : head + 1, :]

            run(pl.multiple_of(number * length, length), length, long_mask, load)
            return carry

        lax.fori_loop(0, batch, long_step, 0)

        def short_load(query_at, head):
            return short_log_ref[query_at, head : head + 1, :]

        run(batch * length, short_length, short_mask_of(docs_ref), short_load)

    forward_call = pl.pallas_call(
        forward,
        out_shape=(
            jax.ShapeDtypeStruct((chunks, rows_all, width), dtype),
            jax.ShapeDtypeStruct((batch, chunks, heads, length), jnp.float32),
            jax.ShapeDtypeStruct((chunks, heads, short_length), jnp.float32),
        ),
        in_specs=[smem, vmem],
        out_specs=(vmem, vmem, vmem),
        name="attention_forward",
    )
    backward_call = pl.pallas_call(
        backward,
        out_shape=(
            jax.ShapeDtypeStruct((chunks, rows_all, 3 * width), dtype),
            jax.ShapeDtypeStruct((2, width), jnp.float32),
        ),
        in_specs=[smem, vmem, vmem, vmem, vmem],
        out_specs=(vmem, vmem),
        name="attention_backward",
    )
    return forward_call, backward_call


def run_layer(tokens, cotangent, docs, batch, length, weights, vectors):
    w_attend, w_merge, w_expand, w_contract = weights
    (
        gain_one,
        shift_one,
        bias_query,
        bias_value,
        bias_merge,
        gain_two,
        shift_two,
        bias_contract,
        bias_expand,
    ) = unpack(vectors)
    rows_all = tokens.shape[0]
    chunks = lax.axis_size("seq")
    width = D // chunks
    forward_call, backward_call = attention_calls(
        chunks, batch, length, rows_all - batch * length, width
    )
    inputs = tokens.astype(jnp.float32)
    normed_one, norm_one_back = jax.vjp(layer_norm, inputs, gain_one, shift_one)
    normed_low = normed_one.astype(jnp.bfloat16)
    joined = jnp.dot(normed_low, w_attend, preferred_element_type=jnp.float32)
    joined_bias = jnp.concatenate([bias_query, jnp.zeros_like(bias_query), bias_value])
    joined_all = (joined + joined_bias).astype(jnp.bfloat16)
    by_heads = exchange(
        joined_all.reshape(rows_all, 3, chunks, width)
        .transpose(2, 0, 1, 3)
        .reshape(chunks, rows_all, 3 * width)
    )
    mixed_heads, long_log, short_log = forward_call(docs, by_heads)
    mixed = exchange(mixed_heads).transpose(1, 0, 2).reshape(rows_all, D)
    middle = inputs + jnp.dot(mixed, w_merge, preferred_element_type=jnp.float32) + bias_merge
    normed_two, norm_two_back = jax.vjp(layer_norm, middle, gain_two, shift_two)
    hidden = normed_two.astype(jnp.bfloat16)
    expanded = jnp.dot(hidden, w_expand, preferred_element_type=jnp.float32) + bias_expand
    activated, gelu_back = jax.vjp(partial(jax.nn.gelu, approximate=True), expanded)
    active_low = activated.astype(jnp.bfloat16)
    output = (
        middle + jnp.dot(active_low, w_contract, preferred_element_type=jnp.float32) + bias_contract
    )
    grad_out = cotangent.astype(jnp.float32)
    contract_bias_grad = jnp.sum(grad_out, axis=0)
    grad_active = contract_cols(cotangent, w_contract)
    (grad_expanded,) = gelu_back(grad_active)
    expand_bias_grad = jnp.sum(grad_expanded, axis=0)
    expanded_low = grad_expanded.astype(jnp.bfloat16)
    grad_hidden = contract_cols(expanded_low, w_expand)
    middle_part, gain_two_grad, shift_two_grad = norm_two_back(grad_hidden)
    grad_middle = grad_out + middle_part
    merge_bias_grad = jnp.sum(grad_middle, axis=0)
    middle_low = grad_middle.astype(jnp.bfloat16)
    grad_mixed = contract_cols(middle_low, w_merge).astype(jnp.bfloat16)
    grad_heads = exchange(grad_mixed.reshape(rows_all, chunks, width).transpose(1, 0, 2))
    joined_heads, head_sums = backward_call(docs, by_heads, grad_heads, long_log, short_log)
    joined_low = (
        exchange(joined_heads)
        .reshape(chunks, rows_all, 3, width)
        .transpose(1, 2, 0, 3)
        .reshape(rows_all, 3 * D)
    )
    bias_sums = lax.dynamic_update_slice_in_dim(
        jnp.zeros((2, D), jnp.float32), head_sums, lax.axis_index("seq") * width, 1
    )
    grad_normed = contract_cols(joined_low, w_attend)
    input_part, gain_one_grad, shift_one_grad = norm_one_back(grad_normed)
    grad_input = grad_middle + input_part
    vector_grad = jnp.concatenate(
        [
            gain_one_grad,
            shift_one_grad,
            bias_sums[0],
            bias_sums[1],
            merge_bias_grad,
            gain_two_grad,
            shift_two_grad,
            contract_bias_grad,
            expand_bias_grad,
        ]
    )
    operands = (
        normed_low,
        joined_low,
        mixed,
        middle_low,
        hidden,
        expanded_low,
        active_low,
        cotangent,
    )
    return output, grad_input, operands, vector_grad


def gather_weights(masters):
    attend, merge, expand, contract = (master.astype(jnp.bfloat16) for master in masters)
    rows = attend.shape[0]
    pieces = contract.shape[0] // rows
    packs = (
        jnp.concatenate([attend, merge], axis=1),
        expand,
        jnp.concatenate([contract[at * rows : (at + 1) * rows] for at in range(pieces)], axis=1),
    )
    seq_count = lax.axis_size("seq")
    rep_count = lax.axis_size("rep")
    whole = [
        lax.all_gather(pack, ("seq", "rep"), axis=0, tiled=False).reshape(
            seq_count, rep_count, rows, pack.shape[1]
        )
        for pack in packs
    ]

    def join(blocks):
        return blocks.transpose(0, 2, 1, 3).reshape(seq_count * rows, -1)

    split = attend.shape[1]
    contract_blocks = whole[2].reshape(seq_count, rep_count, rows, pieces, contract.shape[1])
    return (
        join(whole[0][..., :split]),
        join(whole[0][..., split:]),
        join(whole[1]),
        contract_blocks.transpose(0, 3, 2, 1, 4).reshape(seq_count * pieces * rows, -1),
    )


def local(
    long_input,
    short_input,
    long_cotangent,
    short_cotangent,
    doc_lengths,
    master_attend,
    master_merge,
    master_expand,
    master_contract,
    momentum_attend,
    momentum_merge,
    momentum_expand,
    momentum_contract,
    error_attend,
    error_merge,
    error_expand,
    error_contract,
    factor_attend,
    factor_merge,
    factor_expand,
    factor_contract,
    vector_params,
    vector_momentum,
):
    masters = (master_attend, master_merge, master_expand, master_contract)
    weights = gather_weights(masters)
    seq_index = lax.axis_index("seq")
    rep_index = lax.axis_index("rep")
    rep_count = lax.axis_size("rep")
    _, batch, length, _ = long_input.shape
    tokens = jnp.concatenate([long_input.reshape(-1, D), short_input[0]], axis=0)
    cotangent = jnp.concatenate([long_cotangent.reshape(-1, D), short_cotangent[0]], axis=0)
    output, grad_input, operands, vector_total = run_layer(
        tokens, cotangent, doc_lengths, batch, length, weights, vector_params
    )
    summed = [
        scatter_rows(
            contract_rows(operands[2 * number], operands[2 * number + 1]).astype(jnp.bfloat16)
        )
        for number in range(4)
    ]
    errors = (error_attend, error_merge, error_expand, error_contract)
    factors = (factor_attend, factor_merge, factor_expand, factor_contract)
    momenta = (momentum_attend, momentum_merge, momentum_expand, momentum_contract)
    corrected = [summed[number] + errors[number][0] for number in range(4)]
    heights = [corrected[number].shape[0] for number in range(4)]
    padded = [-(-height // LANES) * LANES for height in heights]
    projected = jnp.concatenate(
        [
            jnp.pad(
                lax.dot_general(
                    factors[number],
                    corrected[number],
                    (((0,), (1,)), ((), ())),
                    precision=HIGH,
                    preferred_element_type=jnp.float32,
                ),
                ((0, 0), (0, padded[number] - heights[number])),
            )
            for number in range(4)
        ],
        axis=1,
    )
    reduced = butterfly_sum(projected, "rep")
    whole_p = gather_stacked(reduced, "seq")
    basis_own = orthonormal(whole_p, padded, 1.0 / rep_count)
    basis_rows = []
    partial_q = []
    offset = 0
    for number in range(4):
        own_rows = basis_own[:, offset : offset + heights[number]]
        offset += padded[number]
        basis_rows.append(own_rows)
        partial_q.append(
            jnp.dot(
                own_rows, corrected[number], precision=HIGH, preferred_element_type=jnp.float32
            )
        )
    rank = projected.shape[0]
    renewed_all = jnp.concatenate(partial_q + [vector_total.reshape(rank, -1)], axis=1)
    renewed_all = butterfly_sum(butterfly_sum(renewed_all, "seq"), "rep")
    renewed_all = renewed_all / rep_count
    updated = []
    new_momenta = []
    new_errors = []
    new_factors = []
    offset = 0
    for number in range(4):
        columns = corrected[number].shape[1]
        renewed = renewed_all[:, offset : offset + columns]
        offset += columns
        approx = contract_rows(basis_rows[number], renewed, HIGH)
        new_errors.append((corrected[number] - approx)[None])
        width = masters[number].shape[1]
        own_block = lax.dynamic_slice_in_dim(approx, rep_index * width, width, 1)
        momentum_next = BETA * momenta[number] + own_block
        new_momenta.append(momentum_next)
        updated.append(masters[number] - RATE_MATRIX * momentum_next)
        new_factors.append(renewed.T)
    vector_grad = renewed_all[:, offset:].reshape(vector_total.shape)
    momenta_vectors = BETA * vector_momentum + vector_grad
    updated_vectors = vector_params - RATE_VECTOR * momenta_vectors
    split = batch * length
    long_output = output[:split].reshape(long_input.shape)
    long_grad = grad_input[:split].reshape(long_input.shape)
    short_output = output[split:].reshape(short_input.shape)
    short_grad = grad_input[split:].reshape(short_input.shape)
    return (
        long_output,
        short_output,
        long_grad,
        short_grad,
        updated[0],
        updated[1],
        updated[2],
        updated[3],
        new_momenta[0],
        new_momenta[1],
        new_momenta[2],
        new_momenta[3],
        new_errors[0],
        new_errors[1],
        new_errors[2],
        new_errors[3],
        new_factors[0],
        new_factors[1],
        new_factors[2],
        new_factors[3],
        updated_vectors,
        momenta_vectors,
    )


def solution(mesh):
    in_specs = (
        P("rep", None, "seq", None),
        P("rep", "seq", None),
        P("rep", None, "seq", None),
        P("rep", "seq", None),
        P("rep", None),
        P("seq", "rep"),
        P("seq", "rep"),
        P("seq", "rep"),
        P("seq", "rep"),
        P("seq", "rep"),
        P("seq", "rep"),
        P("seq", "rep"),
        P("seq", "rep"),
        P("rep", "seq", None),
        P("rep", "seq", None),
        P("rep", "seq", None),
        P("rep", "seq", None),
        P(),
        P(),
        P(),
        P(),
        P(),
        P(),
    )
    out_specs = (
        P("rep", None, "seq", None),
        P("rep", "seq", None),
        P("rep", None, "seq", None),
        P("rep", "seq", None),
        P("seq", "rep"),
        P("seq", "rep"),
        P("seq", "rep"),
        P("seq", "rep"),
        P("seq", "rep"),
        P("seq", "rep"),
        P("seq", "rep"),
        P("seq", "rep"),
        P("rep", "seq", None),
        P("rep", "seq", None),
        P("rep", "seq", None),
        P("rep", "seq", None),
        P(),
        P(),
        P(),
        P(),
        P(),
        P(),
    )
    return jax.shard_map(local, mesh=mesh, in_specs=in_specs, out_specs=out_specs, check_vma=False)
```

```python
from functools import partial

import jax
import jax.numpy as jnp
from jax import lax
from jax.experimental import pallas as pl
from jax.experimental.pallas import tpu as pltpu
from jax.sharding import PartitionSpec as P

D = 768
HEADS = 12
HDIM = 64
LANES = 128


LN_EPS = 1e-05
NORM_EPS = 1e-06
BETA = 0.9
RATE_MATRIX = 0.1
RATE_VECTOR = 0.01
MASKED = -1e30
HIGH = lax.Precision.HIGHEST


def layer_norm(values, gain, shift):
    center = values - jnp.mean(values, axis=-1, keepdims=True)
    spread = jnp.mean(center * center, axis=-1, keepdims=True)
    return center * lax.rsqrt(spread + LN_EPS) * gain + shift


def unpack(vectors):
    head = vectors[: 8 * D].reshape(8, D)
    return (
        head[0],
        head[1],
        head[2],
        head[3],
        head[4],
        head[5],
        head[6],
        head[7],
        vectors[8 * D :],
    )


def orthonormal(gathered, widths, scale):
    rank = gathered.shape[1]

    def over_pieces(values):
        parts = [values[at : at + 1] for at in range(values.shape[0])]
        while len(parts) > 1:
            parts = [left + right for left, right in zip(parts[::2], parts[1::2])]
        return parts[0]

    def kernel(p_ref, basis_ref):
        offset = 0
        for width in widths:
            block = p_ref[:, :, offset : offset + width] * scale
            row_ids = lax.broadcasted_iota(jnp.int32, (1, rank, 1), 1)
            for column_id in range(rank):
                column = block[:, column_id : column_id + 1, :]
                length = over_pieces(jnp.sum(column * column, axis=2, keepdims=True))
                unit = column * lax.rsqrt(length + NORM_EPS)
                inner = over_pieces(jnp.sum(block * unit, axis=2, keepdims=True))
                later = jnp.where(row_ids > column_id, inner, 0.0)
                block = jnp.where(row_ids == column_id, unit, block - later * unit)
            basis_ref[:, offset : offset + width] = block[0]
            offset += width

    return pl.pallas_call(
        kernel, out_shape=jax.ShapeDtypeStruct(gathered.shape[1:], jnp.float32), name="orthonormal"
    )(gathered)


def contract_rows(left, right, precision=None):
    return lax.dot_general(
        left,
        right,
        (((0,), (0,)), ((), ())),
        precision=precision,
        preferred_element_type=jnp.float32,
    )


def contract_cols(left, right, precision=None):
    return lax.dot_general(
        left,
        right,
        (((1,), (1,)), ((), ())),
        precision=precision,
        preferred_element_type=jnp.float32,
    )


def swap_with(values, axis, distance):
    count = lax.axis_size(axis)
    return lax.ppermute(values, axis, [(source, source ^ distance) for source in range(count)])


def butterfly_sum(values, axis, first=1):
    count = lax.axis_size(axis)
    distances = [1 << bit for bit in range(count.bit_length() - 1)]
    for distance in [d for d in distances if d >= first] + [d for d in distances if d < first]:
        values = values + swap_with(values, axis, distance)
    return values


def gather_stacked(values, axis):
    count = lax.axis_size(axis)
    return jnp.stack(
        [values] + [swap_with(values, axis, distance) for distance in range(1, count)]
    )


def halve(blocks, axis_at, distance):
    bit = (lax.axis_index("seq") // distance) % 2
    sent = lax.dynamic_index_in_dim(blocks, 1 - bit, axis_at, keepdims=False)
    kept = lax.dynamic_index_in_dim(blocks, bit, axis_at, keepdims=False)
    received = swap_with(sent, "seq", distance)
    return kept.astype(jnp.float32) + received.astype(jnp.float32)


def scatter_rows(matrix):
    rows, columns = matrix.shape
    if lax.axis_size("seq") != 4:
        return lax.psum_scatter(matrix, "seq", scatter_dimension=0, tiled=True).astype(jnp.float32)
    blocks = matrix.reshape(2, 2, rows // 4, columns)
    middle = columns // 2
    first = halve(blocks[..., :middle], 1, 1).astype(jnp.bfloat16)
    second = halve(blocks[..., middle:], 0, 2).astype(jnp.bfloat16)
    return jnp.concatenate([halve(first, 0, 2), halve(second, 0, 1)], axis=1)


def exchange(values):
    return lax.all_to_all(values, "seq", split_axis=0, concat_axis=0, tiled=True)


def dot_of(left, right, left_dim, right_dim):
    return lax.dot_general(
        left,
        right,
        (((left_dim,), (right_dim,)), ((), ())),
        preferred_element_type=jnp.float32,
    )


def attention_calls(chunks, batch, length, short_length, width, dtype=jnp.bfloat16):
    heads = width // HDIM
    scale = HDIM ** (-0.5)
    rows_all = batch * length + short_length
    smem = pl.BlockSpec(memory_space=pltpu.SMEM)
    vmem = pl.BlockSpec(memory_space=pltpu.VMEM)

    def causal(size):
        key_ids = lax.broadcasted_iota(jnp.int32, (size, size), 0)
        query_ids = lax.broadcasted_iota(jnp.int32, (size, size), 1)
        return key_ids <= query_ids

    def long_mask(scores, key_at, query_at):
        if key_at != query_at:
            return scores
        return jnp.where(causal(length), scores, MASKED)

    def short_mask_of(docs_ref):
        ends = []
        end = 0
        for number in range(docs_ref.shape[1]):
            end = end + docs_ref[0, number]
            ends.append(end)

        def document(position):
            found = jnp.zeros_like(position)
            for end in ends:
                found = found + jnp.where(position >= end, 1, 0)
            return found

        def short_mask(scores, key_at, query_at):
            size = short_length
            key_ids = lax.broadcasted_iota(jnp.int32, (size, 1), 0) + key_at * size
            query_ids = lax.broadcasted_iota(jnp.int32, (1, size), 1) + query_at * size
            allowed = document(key_ids) == document(query_ids)
            if key_at == query_at:
                allowed = allowed & causal(size)
            return jnp.where(allowed, scores, MASKED)

        return short_mask

    def parts_of(ref, first, size, start, head):
        low = start + head * HDIM
        return [ref[chunk, pl.ds(first, size), low : low + HDIM] for chunk in range(chunks)]

    def forward(docs_ref, joined_ref, mixed_ref, long_log_ref, short_log_ref):
        def run(first, size, mask, log_store):
            for query_at in range(chunks):
                pieces = []
                for head in range(heads):
                    low = head * HDIM
                    query = joined_ref[query_at, pl.ds(first, size), low : low + HDIM] * scale
                    keys = parts_of(joined_ref, first, size, width, head)
                    values = parts_of(joined_ref, first, size, 2 * width, head)
                    scores = [
                        mask(dot_of(keys[at], query, 1, 1), at, query_at)
                        for at in range(query_at + 1)
                    ]
                    top = jnp.max(scores[0], axis=0, keepdims=True)
                    for part in scores[1:]:
                        top = jnp.maximum(top, jnp.max(part, axis=0, keepdims=True))
                    expo = [jnp.exp(part - top) for part in scores]
                    total = sum(jnp.sum(part, axis=0, keepdims=True) for part in expo)
                    inverse = 1.0 / total
                    pieces.append(
                        sum(
                            dot_of(values[at], (expo[at] * inverse).astype(dtype), 0, 0)
                            for at in range(query_at + 1)
                        )
                    )
                    log_store(query_at, head, top + jnp.log(total))
                mixed = jnp.concatenate(pieces, axis=0).T
                mixed_ref[query_at, pl.ds(first, size), :] = mixed.astype(dtype)

        def long_step(number, carry):
            def store(query_at, head, log_total):
                long_log_ref[number, query_at, head : head + 1, :] = log_total

            run(pl.multiple_of(number * length, length), length, long_mask, store)
            return carry

        lax.fori_loop(0, batch, long_step, 0)

        def short_store(query_at, head, log_total):
            short_log_ref[query_at, head : head + 1, :] = log_total

        run(batch * length, short_length, short_mask_of(docs_ref), short_store)

    def backward(
        docs_ref, joined_ref, grad_ref, long_log_ref, short_log_ref, out_ref, sums_ref
    ):
        sums_ref[...] = jnp.zeros_like(sums_ref)

        def run(first, size, mask, log_load):
            grad_query = [[] for _ in range(chunks)]
            grad_key = [[] for _ in range(chunks)]
            grad_value = [[] for _ in range(chunks)]
            for head in range(heads):
                keys = parts_of(joined_ref, first, size, width, head)
                values = parts_of(joined_ref, first, size, 2 * width, head)
                queries = parts_of(joined_ref, first, size, 0, head)
                grads = parts_of(grad_ref, first, size, 0, head)
                key_sums = [0.0] * chunks
                value_sums = [0.0] * chunks
                for query_at in range(chunks):
                    query = queries[query_at] * scale
                    grad = grads[query_at]
                    log_total = log_load(query_at, head)
                    soft = []
                    soft_grad = []
                    inner = 0.0
                    for at in range(query_at + 1):
                        scores = mask(dot_of(keys[at], query, 1, 1), at, query_at)
                        soft.append(jnp.exp(scores - log_total))
                        soft_grad.append(dot_of(values[at], grad, 1, 1))
                        inner = inner + jnp.sum(soft[at] * soft_grad[at], axis=0, keepdims=True)
                    query_sum = 0.0
                    for at in range(query_at + 1):
                        score_grad = (soft[at] * (soft_grad[at] - inner)).astype(dtype)
                        query_sum = query_sum + dot_of(keys[at], score_grad, 0, 0)
                        key_sums[at] = key_sums[at] + dot_of(score_grad, query, 1, 0)
                        value_sums[at] = value_sums[at] + dot_of(
                            soft[at].astype(dtype), grad, 1, 0
                        )
                    grad_query[query_at].append(query_sum * scale)
                for at in range(chunks):
                    grad_key[at].append(key_sums[at])
                    grad_value[at].append(value_sums[at])
            for at in range(chunks):
                query_all = jnp.concatenate(grad_query[at], axis=0).T
                value_all = jnp.concatenate(grad_value[at], axis=1)
                sums_ref[0:1, :] += jnp.sum(query_all, axis=0, keepdims=True)
                sums_ref[1:2, :] += jnp.sum(value_all, axis=0, keepdims=True)
                out_ref[at, pl.ds(first, size), :] = jnp.concatenate(
                    [query_all] + grad_key[at] + [value_all], axis=1
                ).astype(dtype)

        def long_step(number, carry):
            def load(query_at, head):
                return long_log_ref[number, query_at, head : head + 1, :]

            run(pl.multiple_of(number * length, length), length, long_mask, load)
            return carry

        lax.fori_loop(0, batch, long_step, 0)

        def short_load(query_at, head):
            return short_log_ref[query_at, head : head + 1, :]

        run(batch * length, short_length, short_mask_of(docs_ref), short_load)

    forward_call = pl.pallas_call(
        forward,
        out_shape=(
            jax.ShapeDtypeStruct((chunks, rows_all, width), dtype),
            jax.ShapeDtypeStruct((batch, chunks, heads, length), jnp.float32),
            jax.ShapeDtypeStruct((chunks, heads, short_length), jnp.float32),
        ),
        in_specs=[smem, vmem],
        out_specs=(vmem, vmem, vmem),
        name="attention_forward",
    )
    backward_call = pl.pallas_call(
        backward,
        out_shape=(
            jax.ShapeDtypeStruct((chunks, rows_all, 3 * width), dtype),
            jax.ShapeDtypeStruct((2, width), jnp.float32),
        ),
        in_specs=[smem, vmem, vmem, vmem, vmem],
        out_specs=(vmem, vmem),
        name="attention_backward",
    )
    return forward_call, backward_call


def run_layer(tokens, cotangent, docs, batch, length, weights, vectors):
    w_attend, w_merge, w_expand, w_contract = weights
    (
        gain_one,
        shift_one,
        bias_query,
        bias_value,
        bias_merge,
        gain_two,
        shift_two,
        bias_contract,
        bias_expand,
    ) = unpack(vectors)
    rows_all = tokens.shape[0]
    chunks = lax.axis_size("seq")
    width = D // chunks
    forward_call, backward_call = attention_calls(
        chunks, batch, length, rows_all - batch * length, width
    )
    inputs = tokens.astype(jnp.float32)
    normed_one, norm_one_back = jax.vjp(layer_norm, inputs, gain_one, shift_one)
    normed_low = normed_one.astype(jnp.bfloat16)
    joined = jnp.dot(normed_low, w_attend, preferred_element_type=jnp.float32)
    joined_bias = jnp.concatenate([bias_query, jnp.zeros_like(bias_query), bias_value])
    joined_all = (joined + joined_bias).astype(jnp.bfloat16)
    by_heads = exchange(
        joined_all.reshape(rows_all, 3, chunks, width)
        .transpose(2, 0, 1, 3)
        .reshape(chunks, rows_all, 3 * width)
    )
    mixed_heads, long_log, short_log = forward_call(docs, by_heads)
    mixed = exchange(mixed_heads).transpose(1, 0, 2).reshape(rows_all, D)
    middle = inputs + jnp.dot(mixed, w_merge, preferred_element_type=jnp.float32) + bias_merge
    normed_two, norm_two_back = jax.vjp(layer_norm, middle, gain_two, shift_two)
    hidden = normed_two.astype(jnp.bfloat16)
    expanded = jnp.dot(hidden, w_expand, preferred_element_type=jnp.float32) + bias_expand
    activated, gelu_back = jax.vjp(partial(jax.nn.gelu, approximate=True), expanded)
    active_low = activated.astype(jnp.bfloat16)
    output = (
        middle + jnp.dot(active_low, w_contract, preferred_element_type=jnp.float32) + bias_contract
    )
    grad_out = cotangent.astype(jnp.float32)
    contract_bias_grad = jnp.sum(grad_out, axis=0)
    grad_active = contract_cols(cotangent, w_contract)
    (grad_expanded,) = gelu_back(grad_active)
    expand_bias_grad = jnp.sum(grad_expanded, axis=0)
    expanded_low = grad_expanded.astype(jnp.bfloat16)
    grad_hidden = contract_cols(expanded_low, w_expand)
    middle_part, gain_two_grad, shift_two_grad = norm_two_back(grad_hidden)
    grad_middle = grad_out + middle_part
    merge_bias_grad = jnp.sum(grad_middle, axis=0)
    middle_low = grad_middle.astype(jnp.bfloat16)
    grad_mixed = contract_cols(middle_low, w_merge).astype(jnp.bfloat16)
    grad_heads = exchange(grad_mixed.reshape(rows_all, chunks, width).transpose(1, 0, 2))
    joined_heads, head_sums = backward_call(docs, by_heads, grad_heads, long_log, short_log)
    joined_low = (
        exchange(joined_heads)
        .reshape(chunks, rows_all, 3, width)
        .transpose(1, 2, 0, 3)
        .reshape(rows_all, 3 * D)
    )
    bias_sums = lax.dynamic_update_slice_in_dim(
        jnp.zeros((2, D), jnp.float32), head_sums, lax.axis_index("seq") * width, 1
    )
    grad_normed = contract_cols(joined_low, w_attend)
    input_part, gain_one_grad, shift_one_grad = norm_one_back(grad_normed)
    grad_input = grad_middle + input_part
    vector_grad = jnp.concatenate(
        [
            gain_one_grad,
            shift_one_grad,
            bias_sums[0],
            bias_sums[1],
            merge_bias_grad,
            gain_two_grad,
            shift_two_grad,
            contract_bias_grad,
            expand_bias_grad,
        ]
    )
    operands = (
        normed_low,
        joined_low,
        mixed,
        middle_low,
        hidden,
        expanded_low,
        active_low,
        cotangent,
    )
    return output, grad_input, operands, vector_grad


def pack_weights(masters):
    attend, merge, expand, contract = (master.astype(jnp.bfloat16) for master in masters)
    rows = attend.shape[0]
    pieces = contract.shape[0] // rows
    return (
        jnp.concatenate([attend, merge], axis=1),
        expand,
        jnp.concatenate([contract[at * rows : (at + 1) * rows] for at in range(pieces)], axis=1),
    )


def gather_plain(masters):
    packs = pack_weights(masters)
    rows = packs[0].shape[0]
    split = masters[0].shape[1]
    pieces = masters[3].shape[0] // rows
    seq_count = lax.axis_size("seq")
    rep_count = lax.axis_size("rep")
    whole = [
        lax.all_gather(pack, ("seq", "rep"), axis=0, tiled=False).reshape(
            seq_count, rep_count, rows, pack.shape[1]
        )
        for pack in packs
    ]

    def join(blocks):
        return blocks.transpose(0, 2, 1, 3).reshape(seq_count * rows, -1)

    contract_blocks = whole[2].reshape(seq_count, rep_count, rows, pieces, masters[3].shape[1])
    return (
        join(whole[0][..., :split]),
        join(whole[0][..., split:]),
        join(whole[1]),
        contract_blocks.transpose(0, 3, 2, 1, 4).reshape(seq_count * pieces * rows, -1),
    )


def spread_pack(pack):
    near = jnp.stack([pack, swap_with(pack, "rep", 2)])
    far = jnp.stack([swap_with(pack, "rep", 4), swap_with(pack, "rep", 6)])
    near = jnp.stack([near, swap_with(near, "seq", 1)])
    far = jnp.stack([far, swap_with(far, "seq", 2)])
    near = jnp.concatenate([near, swap_with(near, "seq", 2)])
    far = jnp.concatenate([far, swap_with(far, "seq", 1)])
    return near, far, swap_with(near, "rep", 1), swap_with(far, "rep", 1)


def place_pack(spread, splits):
    _, _, rows, lanes = spread[0].shape
    here = jnp.stack([lax.axis_index("seq"), lax.axis_index("rep")]).astype(jnp.int32)
    groups = []
    low = 0
    for split in splits:
        widths = split if isinstance(split, tuple) else (split,)
        group = []
        for width in widths:
            group.append((low, width))
            low += width
        groups.append(group)
    count = 8

    def kernel(here_ref, near_ref, far_ref, near_other_ref, far_other_ref, *outs):
        rep = here_ref[1]
        core = rep % 2
        depth = rep // 2
        columns = [None] * count
        for at in range(count // 2):
            low_bit = (at % 2 + depth) % 2
            is_near = (at // 2 + depth // 2) % 2 == 0
            own = jnp.where(is_near, near_ref[0, low_bit], far_ref[0, low_bit])
            other = jnp.where(is_near, near_other_ref[0, low_bit], far_other_ref[0, low_bit])
            columns[2 * at] = jnp.where(core == 0, own, other)
            columns[2 * at + 1] = jnp.where(core == 0, other, own)
        for out_ref, group in zip(outs, groups):
            for number, (start, width) in enumerate(group):
                out_ref[number * rows : (number + 1) * rows, :] = jnp.concatenate(
                    [column[:, start : start + width] for column in columns], axis=1
                )

    def near_map(distance, here_ref):
        return (distance, 0, 0, 0)

    def far_map(distance, here_ref):
        return ((distance % 2) * 2 + distance // 2, 0, 0, 0)

    def out_map(distance, here_ref):
        seq = here_ref[0]
        return ((distance // 2 + seq // 2) % 2 * 2 + (distance + seq) % 2, 0)

    block = (1, 2, rows, lanes)
    shapes = [(len(group) * rows, count * group[0][1]) for group in groups]
    return pl.pallas_call(
        kernel,
        grid_spec=pltpu.PrefetchScalarGridSpec(
            num_scalar_prefetch=1,
            grid=(4,),
            in_specs=[
                pl.BlockSpec(block, near_map),
                pl.BlockSpec(block, far_map),
                pl.BlockSpec(block, near_map),
                pl.BlockSpec(block, far_map),
            ],
            out_specs=[pl.BlockSpec(shape, out_map) for shape in shapes],
        ),
        out_shape=[
            jax.ShapeDtypeStruct((4 * shape[0], shape[1]), jnp.bfloat16) for shape in shapes
        ],
        name="place_weights",
    )(here, *spread)


def gather_weights(masters):
    if lax.axis_size("seq") != 4 or lax.axis_size("rep") != 8:
        return gather_plain(masters)
    packs = pack_weights(masters)
    pieces = masters[3].shape[0] // masters[0].shape[0]
    attend, merge = place_pack(
        spread_pack(packs[0]), (masters[0].shape[1], masters[1].shape[1])
    )
    (expand,) = place_pack(spread_pack(packs[1]), (masters[2].shape[1],))
    (contract,) = place_pack(spread_pack(packs[2]), ((masters[3].shape[1],) * pieces,))
    return attend, merge, expand, contract


def local(
    long_input,
    short_input,
    long_cotangent,
    short_cotangent,
    doc_lengths,
    master_attend,
    master_merge,
    master_expand,
    master_contract,
    momentum_attend,
    momentum_merge,
    momentum_expand,
    momentum_contract,
    error_attend,
    error_merge,
    error_expand,
    error_contract,
    factor_attend,
    factor_merge,
    factor_expand,
    factor_contract,
    vector_params,
    vector_momentum,
):
    masters = (master_attend, master_merge, master_expand, master_contract)
    weights = gather_weights(masters)
    seq_index = lax.axis_index("seq")
    rep_index = lax.axis_index("rep")
    rep_count = lax.axis_size("rep")
    _, batch, length, _ = long_input.shape
    tokens = jnp.concatenate([long_input.reshape(-1, D), short_input[0]], axis=0)
    cotangent = jnp.concatenate([long_cotangent.reshape(-1, D), short_cotangent[0]], axis=0)
    output, grad_input, operands, vector_total = run_layer(
        tokens, cotangent, doc_lengths, batch, length, weights, vector_params
    )
    summed = [
        scatter_rows(
            contract_rows(operands[2 * number], operands[2 * number + 1]).astype(jnp.bfloat16)
        )
        for number in range(4)
    ]
    errors = (error_attend, error_merge, error_expand, error_contract)
    factors = (factor_attend, factor_merge, factor_expand, factor_contract)
    momenta = (momentum_attend, momentum_merge, momentum_expand, momentum_contract)
    corrected = [summed[number] + errors[number][0] for number in range(4)]
    heights = [corrected[number].shape[0] for number in range(4)]
    padded = [-(-height // LANES) * LANES for height in heights]
    projected = jnp.concatenate(
        [
            jnp.pad(
                lax.dot_general(
                    factors[number],
                    corrected[number],
                    (((0,), (1,)), ((), ())),
                    precision=HIGH,
                    preferred_element_type=jnp.float32,
                ),
                ((0, 0), (0, padded[number] - heights[number])),
            )
            for number in range(4)
        ],
        axis=1,
    )
    reduced = butterfly_sum(projected, "rep")
    whole_p = gather_stacked(reduced, "seq")
    basis_own = orthonormal(whole_p, padded, 1.0 / rep_count)
    basis_rows = []
    partial_q = []
    offset = 0
    for number in range(4):
        own_rows = basis_own[:, offset : offset + heights[number]]
        offset += padded[number]
        basis_rows.append(own_rows)
        partial_q.append(
            jnp.dot(
                own_rows, corrected[number], precision=HIGH, preferred_element_type=jnp.float32
            )
        )
    rank = projected.shape[0]
    renewed_all = jnp.concatenate(partial_q + [vector_total.reshape(rank, -1)], axis=1)
    middle = renewed_all.shape[1] // 2 // LANES * LANES
    renewed_all = jnp.concatenate(
        [
            butterfly_sum(butterfly_sum(renewed_all[:, :middle], "seq"), "rep"),
            butterfly_sum(butterfly_sum(renewed_all[:, middle:], "rep", 2), "seq"),
        ],
        axis=1,
    )
    renewed_all = renewed_all / rep_count
    updated = []
    new_momenta = []
    new_errors = []
    new_factors = []
    offset = 0
    for number in range(4):
        columns = corrected[number].shape[1]
        renewed = renewed_all[:, offset : offset + columns]
        offset += columns
        approx = contract_rows(basis_rows[number], renewed, HIGH)
        new_errors.append((corrected[number] - approx)[None])
        width = masters[number].shape[1]
        own_block = lax.dynamic_slice_in_dim(approx, rep_index * width, width, 1)
        momentum_next = BETA * momenta[number] + own_block
        new_momenta.append(momentum_next)
        updated.append(masters[number] - RATE_MATRIX * momentum_next)
        new_factors.append(renewed.T)
    vector_grad = renewed_all[:, offset:].reshape(vector_total.shape)
    momenta_vectors = BETA * vector_momentum + vector_grad
    updated_vectors = vector_params - RATE_VECTOR * momenta_vectors
    split = batch * length
    long_output = output[:split].reshape(long_input.shape)
    long_grad = grad_input[:split].reshape(long_input.shape)
    short_output = output[split:].reshape(short_input.shape)
    short_grad = grad_input[split:].reshape(short_input.shape)
    return (
        long_output,
        short_output,
        long_grad,
        short_grad,
        updated[0],
        updated[1],
        updated[2],
        updated[3],
        new_momenta[0],
        new_momenta[1],
        new_momenta[2],
        new_momenta[3],
        new_errors[0],
        new_errors[1],
        new_errors[2],
        new_errors[3],
        new_factors[0],
        new_factors[1],
        new_factors[2],
        new_factors[3],
        updated_vectors,
        momenta_vectors,
    )


def solution(mesh):
    in_specs = (
        P("rep", None, "seq", None),
        P("rep", "seq", None),
        P("rep", None, "seq", None),
        P("rep", "seq", None),
        P("rep", None),
        P("seq", "rep"),
        P("seq", "rep"),
        P("seq", "rep"),
        P("seq", "rep"),
        P("seq", "rep"),
        P("seq", "rep"),
        P("seq", "rep"),
        P("seq", "rep"),
        P("rep", "seq", None),
        P("rep", "seq", None),
        P("rep", "seq", None),
        P("rep", "seq", None),
        P(),
        P(),
        P(),
        P(),
        P(),
        P(),
    )
    out_specs = (
        P("rep", None, "seq", None),
        P("rep", "seq", None),
        P("rep", None, "seq", None),
        P("rep", "seq", None),
        P("seq", "rep"),
        P("seq", "rep"),
        P("seq", "rep"),
        P("seq", "rep"),
        P("seq", "rep"),
        P("seq", "rep"),
        P("seq", "rep"),
        P("seq", "rep"),
        P("rep", "seq", None),
        P("rep", "seq", None),
        P("rep", "seq", None),
        P("rep", "seq", None),
        P(),
        P(),
        P(),
        P(),
        P(),
        P(),
    )
    return jax.shard_map(local, mesh=mesh, in_specs=in_specs, out_specs=out_specs, check_vma=False)
```
